512 devices in a mesh: ctx: 128 (over z, x, core), head: 4 (over y).
Axes of the slice: x: 4, y: 4, z: 16, core: 2. Of those that a mesh axis runs over, the one named last changes fastest.
Arguments:
- queries: bfloat16 [512, 64, 128], P('ctx', 'head'), may hold values from -24 to 24
- cache_keys: bfloat16 [32768, 8, 128], P('ctx', 'head'), may hold values from -24 to 24
- cache_values: bfloat16 [32768, 8, 128], P('ctx', 'head'), may hold values from -6 to 6
- new_keys: bfloat16 [512, 8, 128], P('ctx', 'head'), may hold values from -6 to 6
- new_values: bfloat16 [512, 8, 128], P('ctx', 'head'), may hold values from -6 to 6
- frame_of_slot: int32 [128], P('ctx'), may hold values from 0 to 127, each once
- slopes: float32 [64], P('head'), may hold values from 0.002 to 0.1
Outputs:
- attended: bfloat16 [512, 8192], P('ctx')
The draws below stay inside these ranges and needn't reach their ends.
Inputs may be any that keep to these rules, and one draw needn't show every extreme that they name: `frame_of_slot`: each frame number 0 to 127 stands in exactly one slot.
All inputs are finite; a program needn't handle non-finite values.
Results may differ from the reference program's by a relative error of at most 0.0085.
Values may be sent and summed in bfloat16 or wider, within the bound.
No kernel may reach another device: no remote copies, remote signals or barrier semaphores. Data moves between devices by JAX's collectives and lax.ppermute only.
A program may use at most 64 MiB of HBM per device.

```python
import math
import jax
import jax.numpy as jnp
from jax import lax

HEADS = 64
KVH = 8
HD = 128
FRAME = 256
QTOK = 512
CACHE_FRAMES = 128
CACHE = 32768


def draw_queries(key, part):
    values = jnp.clip(jax.random.normal(jax.random.fold_in(key, 1), (QTOK, HEADS, HD), jnp.float32), -5.0, 5.0)
    return values.astype(jnp.bfloat16)


def draw_cache_keys(key, part):
    values = jnp.clip(jax.random.normal(jax.random.fold_in(key, 2), (CACHE, KVH, HD), jnp.float32), -5.0, 5.0)
    return values.astype(jnp.bfloat16)


def level_of(rng, dims, pieces, low, high):
    factor_of = 1.0
    for position, blocks in pieces:
        steps = jax.random.uniform(jax.random.fold_in(jax.random.fold_in(rng, 6), position), (blocks,), jnp.float32, low / len(pieces), high / len(pieces))
        factor_of = factor_of * jnp.repeat(jnp.exp(steps), dims[position] // blocks).reshape((-1,) + (1,) * (len(dims) - 1 - position))
    return factor_of


def noise(key, extent, width, reach, split=(), kind=jnp.bfloat16):
    values = width * jax.random.normal(key, extent, jnp.float32)
    if split:
        values = values * level_of(key, extent, split, -0.22, 0.18)
    return jnp.clip(values, -reach, reach).astype(kind)


def setup_inputs(seed: int = 0) -> dict:
    keys = jax.random.split(jax.random.key(seed), 8)
    return {
        "queries": draw_queries(jax.random.fold_in(keys[7], 71), 0),
        "cache_keys": draw_cache_keys(jax.random.fold_in(keys[7], 71), 0),
        "cache_values": noise(keys[2], (CACHE, KVH, HD), 1.0, 6.0, ((0, 128), (1, 4))),
        "new_keys": noise(keys[3], (QTOK, KVH, HD), 1.0, 6.0, ((0, 128), (1, 4))),
        "new_values": noise(keys[4], (QTOK, KVH, HD), 1.0, 6.0, ((0, 128), (1, 4))),
        "frame_of_slot": jax.random.permutation(keys[5], CACHE_FRAMES).astype(jnp.int32),
        "slopes": jnp.clip(jnp.exp(math.log(0.1) - 3.912023 * jax.random.uniform(keys[6], (HEADS,), jnp.float32) ** level_of(keys[6], (HEADS,), ((0, 4),), -0.2, 0.2)), 0.002, 0.1),
    }


def reference(queries, cache_keys, cache_values, new_keys, new_values, frame_of_slot, slopes):
    group = HEADS // KVH
    scale = 1.0 / (HD ** 0.5)
    qpos = jnp.arange(QTOK, dtype=jnp.int32)
    qframe = (CACHE_FRAMES + qpos // FRAME).astype(jnp.float32)
    cframe = jnp.repeat(frame_of_slot, FRAME).astype(jnp.float32)
    nframe = qframe
    block = 8 * FRAME
    blocks = CACHE // block
    qall = jnp.transpose(queries.reshape(QTOK, KVH, group, HD), (1, 0, 2, 3))
    kall = jnp.transpose(cache_keys, (1, 0, 2)).reshape(KVH, blocks, block, HD)
    vall = jnp.transpose(cache_values, (1, 0, 2)).reshape(KVH, blocks, block, HD)
    knew = jnp.transpose(new_keys, (1, 0, 2))
    vnew = jnp.transpose(new_values, (1, 0, 2))
    slope_all = slopes.reshape(KVH, group)
    cframe_blocks = cframe.reshape(blocks, block)
    causal = qpos[None, :] <= qpos[:, None]

    def update(state, score, values):
        acc, high, total = state
        new_high = jnp.maximum(high, jnp.max(score, axis=-1))
        corr = jnp.exp(high - new_high)
        expo = jnp.exp(score - new_high[..., None])
        total = total * corr + jnp.sum(expo, axis=-1)
        weight = lax.optimization_barrier(expo.astype(jnp.bfloat16)).astype(jnp.float32)
        acc = acc * corr[..., None] + jnp.einsum("tqk,kd->tqd", weight, values.astype(jnp.float32))
        return acc, new_high, total

    def one_group(items):
        qg, kg, vg, kn, vn, sl = items
        q32 = qg.astype(jnp.float32)
        init = (jnp.zeros((QTOK, group, HD), jnp.float32), jnp.full((QTOK, group), -1e30, jnp.float32), jnp.zeros((QTOK, group), jnp.float32))

        def scan_step(state, xs):
            kb, vb, fb = xs
            score = jnp.einsum("tqd,kd->tqk", q32, kb.astype(jnp.float32)) * scale
            score = score - sl[None, :, None] * (qframe[:, None, None] - fb[None, None, :])
            return update(state, score, vb), None

        state, _ = lax.scan(scan_step, init, (kg, vg, cframe_blocks))
        score = jnp.einsum("tqd,kd->tqk", q32, kn.astype(jnp.float32)) * scale
        score = score - sl[None, :, None] * (qframe[:, None, None] - nframe[None, None, :])
        score = jnp.where(causal[:, None, :], score, -1e30)
        acc, high, total = update(state, score, vn)
        return acc / total[..., None]

    outs = lax.map(one_group, (qall, kall, vall, knew, vnew, slope_all))
    return jnp.transpose(outs, (1, 0, 2, 3)).reshape(QTOK, HEADS * HD).astype(jnp.bfloat16)
```

```python
import functools
import math

import jax
import jax.numpy as jnp
from jax import lax
from jax.experimental import pallas as pl
from jax.experimental.pallas import tpu as pltpu
from jax.sharding import Mesh, PartitionSpec as P

FRAME = 256
TAIL = 16
LOG2E = math.log2(math.e)
GRID = (16, 4, 2)
OFFSETS = (0, 1, -1, 2)
ATTEND_VMEM = 24 << 20
MERGE_VMEM = 4 << 20


def shifted(value, axis, steps):
    count = lax.axis_size(axis)
    pairs = [(source, (source + steps) % count) for source in range(count)]
    return lax.ppermute(value, axis, pairs)


def attend(cache_frames, kv0, kv1, kv2, kv3, q_ref, slope_ref, out_ref):
    kvs = (kv0, kv1, kv2, kv3)
    zs, rows, heads, width = q_ref.shape
    cores = kv0.shape[0]
    groups = kv0.shape[2]
    group = heads // groups
    keys = kv0.shape[3] - TAIL
    xs = len(kvs)
    z, x, c = lax.axis_index("z"), lax.axis_index("x"), lax.axis_index("c")
    per_z = xs * cores * rows
    zb = FRAME // per_z
    zrows = rows * group
    block = zb * zrows
    scale = LOG2E / width**0.5
    shards = xs * cores

    new = shards * TAIL
    row = lax.broadcasted_iota(jnp.int32, (block, new), 0)
    col = lax.broadcasted_iota(jnp.int32, (block, new), 1)
    slot = col // TAIL
    within = col % TAIL
    source = lax.rem(x + xs - jnp.zeros_like(slot), xs)
    for i, off in enumerate(OFFSETS):
        source = jnp.where(slot // cores == i, lax.rem(x + xs - off, xs), source)
    kpos = z * per_z + (source * cores + slot % cores) * rows + within
    lane = lax.broadcasted_iota(jnp.int32, (zrows, width), 1)
    sub = lax.broadcasted_iota(jnp.int32, (zrows, width), 0)
    tail_row = lax.broadcasted_iota(jnp.int32, (TAIL, width), 0)
    new_frame = (cache_frames + z * per_z // FRAME).astype(jnp.float32)

    for b in range(zs // zb):
        qpos = (b * zb + row // zrows) * per_z + (x * cores + c) * rows + (row // group) % rows
        visible = (within < rows) & (kpos <= qpos)
        qframe = float(cache_frames + b)
        lse_rows = jnp.zeros((zb, width), jnp.float32)
        q_all = q_ref[b * zb : (b + 1) * zb].astype(jnp.float32).reshape(zb * rows, heads, width)
        for h in range(groups):
            slope = slope_ref[h]
            q = q_all[:, h * group : (h + 1) * group, :].reshape(block, width).astype(jnp.bfloat16)
            scores = []
            for a in range(xs):
                for i in range(cores):
                    k = kvs[a][i, 0, h, :keys, :]
                    frame = kvs[a][i, 0, h, keys:, :].astype(jnp.float32)[TAIL // 2 :, :]
                    bias = slope * (qframe - frame) * -LOG2E
                    bias = jnp.concatenate([bias] * (keys // width), axis=1)
                    s = lax.dot_general(q, k, (((1,), (1,)), ((), ())), preferred_element_type=jnp.float32)
                    t = s.reshape(block // group, group, keys) * scale + bias[None]
                    scores.append(t.reshape(block, keys))
            kn = jnp.concatenate([kvs[a][i, 0, h, keys:, :] for a in range(xs) for i in range(cores)], axis=0)
            vn = jnp.concatenate([kvs[a][i, 1, h, keys:, :] for a in range(xs) for i in range(cores)], axis=0)
            bias = slope * (qframe - new_frame) * -LOG2E
            s = lax.dot_general(q, kn, (((1,), (1,)), ((), ())), preferred_element_type=jnp.float32)
            t = (s.reshape(block // group, group, new) * scale + bias[None]).reshape(block, new)
            t_new = jnp.where(visible, t, -1e30)
            top = functools.reduce(jnp.maximum, scores)
            top = functools.reduce(jnp.maximum, [top[:, i : i + new] for i in range(0, keys, new)])
            high = jnp.max(jnp.maximum(top, t_new), axis=1, keepdims=True)
            p_new = jnp.exp2(t_new - high)
            acc = jnp.dot(p_new.astype(jnp.bfloat16), vn, preferred_element_type=jnp.float32)
            total = p_new
            for j, t in enumerate(scores):
                p = jnp.exp2(t - high)
                for i in range(0, keys, new):
                    total = total + p[:, i : i + new]
                v = kvs[j // cores][j % cores, 1, h, :keys, :]
                acc = acc + jnp.dot(p.astype(jnp.bfloat16), v, preferred_element_type=jnp.float32)
            total = jnp.sum(total, axis=1, keepdims=True)
            out = (acc / total).astype(jnp.bfloat16)
            out_ref[b * zb : (b + 1) * zb, h * zrows : (h + 1) * zrows, :] = out.reshape(zb, zrows, width)
            lse = jnp.broadcast_to(high + jnp.log2(total), (block, width)).reshape(zb, zrows, width)
            lse_rows = lse_rows + jnp.sum(jnp.where((sub + h * zrows == lane)[None], lse, 0.0), axis=1)
        first = lse_rows.astype(jnp.bfloat16).astype(jnp.float32)
        second = (lse_rows - first).astype(jnp.bfloat16).astype(jnp.float32)
        third = lse_rows - first - second
        for i in range(zb):
            tail = jnp.where(tail_row == 0, first[i : i + 1], 0.0)
            tail = jnp.where(tail_row == 1, second[i : i + 1], tail)
            tail = jnp.where(tail_row == 2, third[i : i + 1], tail)
            out_ref[b * zb + i, groups * zrows :, :] = tail.astype(jnp.bfloat16)


def merge(rows, groups, in_ref, out_ref, scratch):
    zs, _, width = in_ref.shape
    count = in_ref.shape[1] - TAIL
    group = count // (rows * groups)
    lse = []
    for s in range(zs):
        tail = in_ref[s, count:, :].astype(jnp.float32)
        lse.append(tail[0:1] + tail[1:2] + tail[2:3])
    lse = jnp.concatenate(lse, axis=0)
    weight = jnp.exp2(lse - jnp.max(lse, axis=0, keepdims=True))
    weight = weight / jnp.sum(weight, axis=0, keepdims=True)
    weight = jnp.concatenate([weight, jnp.zeros((width - zs, width), jnp.float32)], axis=0).T
    acc = jnp.zeros((count, width), jnp.float32)
    for s in range(zs):
        acc = acc + weight[:count, s : s + 1] * in_ref[s, :count, :].astype(jnp.float32)
    scratch[...] = acc.reshape(groups, rows, group, width)
    for h in range(groups):
        for g in range(group):
            at = (h * group + g) * width
            out_ref[:, at : at + width] = scratch[h, :, g, :].astype(jnp.bfloat16)


def on_device(queries, cache_keys, cache_values, new_keys, new_values, frame_of_slot, slopes):
    rows, heads, width = queries.shape
    keys, groups, _ = cache_keys.shape
    group = heads // groups
    zs, xs, cs = (lax.axis_size(a) for a in ("z", "x", "c"))
    cache_frames = zs * xs * cs * frame_of_slot.shape[0]
    vmem = pl.BlockSpec(memory_space=pltpu.VMEM)

    frame = jnp.broadcast_to(frame_of_slot.astype(jnp.bfloat16)[0], (groups, TAIL // 2, width))
    pad = jnp.zeros((groups, TAIL // 2 - rows, width), jnp.bfloat16)

    def side(cached, new):
        return jnp.concatenate([cached.transpose(1, 0, 2), new.transpose(1, 0, 2), pad, frame], axis=1)

    packed = jnp.stack([side(cache_keys, new_keys), side(cache_values, new_values)])
    own = lax.all_gather(packed, "c")
    blocks = [own if off == 0 else shifted(own, "x", off) for off in OFFSETS]
    q_all = lax.all_gather(queries, "z")
    slope = jnp.broadcast_to(slopes.reshape(groups, group, 1), (groups, group, width))
    chunk = groups * group * rows + TAIL
    partial = pl.pallas_call(
        functools.partial(attend, cache_frames),
        out_shape=jax.ShapeDtypeStruct((zs, chunk, width), jnp.bfloat16),
        in_specs=[vmem] * 6,
        out_specs=vmem,
        compiler_params=pltpu.CompilerParams(vmem_limit_bytes=ATTEND_VMEM),
        name="attend",
    )(*blocks, q_all, slope)
    landed = lax.all_to_all(partial, "z", 0, 0)
    result = pl.pallas_call(
        functools.partial(merge, rows, groups),
        out_shape=jax.ShapeDtypeStruct((rows, heads * width), jnp.bfloat16),
        in_specs=[vmem],
        out_specs=vmem,
        scratch_shapes=[pltpu.VMEM((groups, rows, group, width), jnp.float32)],
        compiler_params=pltpu.CompilerParams(vmem_limit_bytes=MERGE_VMEM),
        name="merge",
    )(landed)
    return lax.all_gather(result, "head", axis=1, tiled=True)


def solution(mesh):
    heads = mesh.devices.shape[1]
    fine = Mesh(mesh.devices.reshape(*GRID, heads), ("z", "x", "c", "head"))
    ctx = ("z", "x", "c")
    return jax.shard_map(
        on_device,
        mesh=fine,
        in_specs=(P(ctx, "head", None),) * 5 + (P(ctx), P("head")),
        out_specs=P(ctx, None),
        check_vma=False,
    )
```

```python
import functools
import math

import jax
import jax.numpy as jnp
from jax import lax
from jax.experimental import pallas as pl
from jax.experimental.pallas import tpu as pltpu
from jax.sharding import Mesh, PartitionSpec as P

FRAME = 256
TAIL = 16
LOG2E = math.log2(math.e)
GRID = (16, 4, 2)
OFFSETS = (0, 1, -1, 2)
ATTEND_VMEM = 24 << 20
MERGE_VMEM = 4 << 20


def shifted(value, axis, steps):
    count = lax.axis_size(axis)
    pairs = [(source, (source + steps) % count) for source in range(count)]
    return lax.ppermute(value, axis, pairs)


def spread(value, axis):
    copies = jnp.broadcast_to(value, (lax.axis_size(axis), *value.shape))
    return lax.all_to_all(copies, axis, 0, 0)


def attend(cache_frames, kv0, kv1, kv2, kv3, q_ref, slope_ref, out_ref):
    kvs = (kv0, kv1, kv2, kv3)
    zs, rows, heads, width = q_ref.shape
    cores = kv0.shape[0]
    groups = kv0.shape[2]
    group = heads // groups
    keys = kv0.shape[3] - TAIL
    xs = len(kvs)
    z, x, c = lax.axis_index("z"), lax.axis_index("x"), lax.axis_index("c")
    per_z = xs * cores * rows
    zb = FRAME // per_z
    zrows = rows * group
    block = zb * zrows
    scale = LOG2E / width**0.5
    shards = xs * cores

    new = shards * TAIL
    row = lax.broadcasted_iota(jnp.int32, (block, new), 0)
    col = lax.broadcasted_iota(jnp.int32, (block, new), 1)
    slot = col // TAIL
    within = col % TAIL
    source = lax.rem(x + xs - jnp.zeros_like(slot), xs)
    for i, off in enumerate(OFFSETS):
        source = jnp.where(slot // cores == i, lax.rem(x + xs - off, xs), source)
    kpos = z * per_z + (source * cores + slot % cores) * rows + within
    lane = lax.broadcasted_iota(jnp.int32, (zrows, width), 1)
    sub = lax.broadcasted_iota(jnp.int32, (zrows, width), 0)
    tail_row = lax.broadcasted_iota(jnp.int32, (TAIL, width), 0)
    new_frame = (cache_frames + z * per_z // FRAME).astype(jnp.float32)

    for b in range(zs // zb):
        qpos = (b * zb + row // zrows) * per_z + (x * cores + c) * rows + (row // group) % rows
        visible = (within < rows) & (kpos <= qpos)
        qframe = float(cache_frames + b)
        lse_rows = jnp.zeros((zb, width), jnp.float32)
        q_all = q_ref[b * zb : (b + 1) * zb].astype(jnp.float32).reshape(zb * rows, heads, width)
        for h in range(groups):
            slope = slope_ref[h]
            q = q_all[:, h * group : (h + 1) * group, :].reshape(block, width).astype(jnp.bfloat16)
            scores = []
            for a in range(xs):
                for i in range(cores):
                    k = kvs[a][i, 0, h, :keys, :]
                    frame = kvs[a][i, 0, h, keys:, :].astype(jnp.float32)[TAIL // 2 :, :]
                    bias = slope * (qframe - frame) * -LOG2E
                    bias = jnp.concatenate([bias] * (keys // width), axis=1)
                    s = lax.dot_general(q, k, (((1,), (1,)), ((), ())), preferred_element_type=jnp.float32)
                    t = s.reshape(block // group, group, keys) * scale + bias[None]
                    scores.append(t.reshape(block, keys))
            kn = jnp.concatenate([kvs[a][i, 0, h, keys:, :] for a in range(xs) for i in range(cores)], axis=0)
            vn = jnp.concatenate([kvs[a][i, 1, h, keys:, :] for a in range(xs) for i in range(cores)], axis=0)
            bias = slope * (qframe - new_frame) * -LOG2E
            s = lax.dot_general(q, kn, (((1,), (1,)), ((), ())), preferred_element_type=jnp.float32)
            t = (s.reshape(block // group, group, new) * scale + bias[None]).reshape(block, new)
            t_new = jnp.where(visible, t, -1e30)
            top = functools.reduce(jnp.maximum, scores)
            top = functools.reduce(jnp.maximum, [top[:, i : i + new] for i in range(0, keys, new)])
            high = jnp.max(jnp.maximum(top, t_new), axis=1, keepdims=True)
            p_new = jnp.exp2(t_new - high)
            acc = jnp.dot(p_new.astype(jnp.bfloat16), vn, preferred_element_type=jnp.float32)
            total = p_new
            for j, t in enumerate(scores):
                p = jnp.exp2(t - high)
                for i in range(0, keys, new):
                    total = total + p[:, i : i + new]
                v = kvs[j // cores][j % cores, 1, h, :keys, :]
                acc = acc + jnp.dot(p.astype(jnp.bfloat16), v, preferred_element_type=jnp.float32)
            total = jnp.sum(total, axis=1, keepdims=True)
            out = (acc / total).astype(jnp.bfloat16)
            out_ref[b * zb : (b + 1) * zb, h * zrows : (h + 1) * zrows, :] = out.reshape(zb, zrows, width)
            lse = jnp.broadcast_to(high + jnp.log2(total), (block, width)).reshape(zb, zrows, width)
            lse_rows = lse_rows + jnp.sum(jnp.where((sub + h * zrows == lane)[None], lse, 0.0), axis=1)
        first = lse_rows.astype(jnp.bfloat16).astype(jnp.float32)
        second = (lse_rows - first).astype(jnp.bfloat16).astype(jnp.float32)
        third = lse_rows - first - second
        for i in range(zb):
            tail = jnp.where(tail_row == 0, first[i : i + 1], 0.0)
            tail = jnp.where(tail_row == 1, second[i : i + 1], tail)
            tail = jnp.where(tail_row == 2, third[i : i + 1], tail)
            out_ref[b * zb + i, groups * zrows :, :] = tail.astype(jnp.bfloat16)


def merge(rows, groups, in_ref, out_ref, scratch):
    zs, _, width = in_ref.shape
    count = in_ref.shape[1] - TAIL
    group = count // (rows * groups)
    lse = []
    for s in range(zs):
        tail = in_ref[s, count:, :].astype(jnp.float32)
        lse.append(tail[0:1] + tail[1:2] + tail[2:3])
    lse = jnp.concatenate(lse, axis=0)
    weight = jnp.exp2(lse - jnp.max(lse, axis=0, keepdims=True))
    weight = weight / jnp.sum(weight, axis=0, keepdims=True)
    weight = jnp.concatenate([weight, jnp.zeros((width - zs, width), jnp.float32)], axis=0).T
    acc = jnp.zeros((count, width), jnp.float32)
    for s in range(zs):
        acc = acc + weight[:count, s : s + 1] * in_ref[s, :count, :].astype(jnp.float32)
    scratch[...] = acc.reshape(groups, rows, group, width)
    for h in range(groups):
        for g in range(group):
            at = (h * group + g) * width
            out_ref[:, at : at + width] = scratch[h, :, g, :].astype(jnp.bfloat16)


def on_device(queries, cache_keys, cache_values, new_keys, new_values, frame_of_slot, slopes):
    rows, heads, width = queries.shape
    keys, groups, _ = cache_keys.shape
    group = heads // groups
    zs, xs, cs = (lax.axis_size(a) for a in ("z", "x", "c"))
    cache_frames = zs * xs * cs * frame_of_slot.shape[0]
    vmem = pl.BlockSpec(memory_space=pltpu.VMEM)

    frame = jnp.broadcast_to(frame_of_slot.astype(jnp.bfloat16)[0], (groups, TAIL // 2, width))
    pad = jnp.zeros((groups, TAIL // 2 - rows, width), jnp.bfloat16)

    def side(cached, new):
        return jnp.concatenate([cached.transpose(1, 0, 2), new.transpose(1, 0, 2), pad, frame], axis=1)

    packed = jnp.stack([side(cache_keys, new_keys), side(cache_values, new_values)])
    own = lax.all_gather(packed, "c")
    blocks = [own if off == 0 else shifted(own, "x", off) for off in OFFSETS]
    q_all = spread(queries, "z")
    slope = jnp.broadcast_to(slopes.reshape(groups, group, 1), (groups, group, width))
    chunk = groups * group * rows + TAIL
    partial = pl.pallas_call(
        functools.partial(attend, cache_frames),
        out_shape=jax.ShapeDtypeStruct((zs, chunk, width), jnp.bfloat16),
        in_specs=[vmem] * 6,
        out_specs=vmem,
        compiler_params=pltpu.CompilerParams(vmem_limit_bytes=ATTEND_VMEM),
        name="attend",
    )(*blocks, q_all, slope)
    landed = lax.all_to_all(partial, "z", 0, 0)
    result = pl.pallas_call(
        functools.partial(merge, rows, groups),
        out_shape=jax.ShapeDtypeStruct((rows, heads * width), jnp.bfloat16),
        in_specs=[vmem],
        out_specs=vmem,
        scratch_shapes=[pltpu.VMEM((groups, rows, group, width), jnp.float32)],
        compiler_params=pltpu.CompilerParams(vmem_limit_bytes=MERGE_VMEM),
        name="merge",
    )(landed)
    return jnp.concatenate(list(spread(result, "head")), axis=1)


def solution(mesh):
    heads = mesh.devices.shape[1]
    fine = Mesh(mesh.devices.reshape(*GRID, heads), ("z", "x", "c", "head"))
    ctx = ("z", "x", "c")
    return jax.shard_map(
        on_device,
        mesh=fine,
        in_specs=(P(ctx, "head", None),) * 5 + (P(ctx), P("head")),
        out_specs=P(ctx, None),
        check_vma=False,
    )
```

```python
import functools
import math

import jax
import jax.numpy as jnp
from jax import lax
from jax.experimental import pallas as pl
from jax.experimental.pallas import tpu as pltpu
from jax.sharding import Mesh, PartitionSpec as P


FRAME = 256
TAIL = 8
OFFSETS = (0, 1, -1, 2)
LOG2E = math.log2(math.e)
GRID = (16, 4, 2)
ATTEND_VMEM = 24 << 20
MERGE_VMEM = 4 << 20


def shifted(value, axis, steps):
    count = lax.axis_size(axis)
    pairs = [(source, (source + steps) % count) for source in range(count)]
    return lax.ppermute(value, axis, pairs)


def spread(value, axis):
    copies = jnp.broadcast_to(value, (lax.axis_size(axis), *value.shape))
    return lax.all_to_all(copies, axis, 0, 0)


def attend(cache_frames, kv0, kv1, kv2, kv3, q_ref, slope_ref, out_ref):
    kvs = (kv0, kv1, kv2, kv3)
    zs, rows, heads, width = q_ref.shape
    cores, _, groups, keys, _ = kv0.shape
    keys -= TAIL
    xs = len(kvs)
    group = heads // groups
    z, x, c = lax.axis_index("z"), lax.axis_index("x"), lax.axis_index("c")
    shards = [(ref, i) for ref in kvs for i in range(cores)]
    per_z = len(shards) * rows
    zb = FRAME // per_z
    zrows = rows * group
    block = zb * zrows
    scale = LOG2E / width**0.5

    row = lax.broadcasted_iota(jnp.int32, (block, width), 0)
    col = lax.broadcasted_iota(jnp.int32, (block, width), 1)
    slot = col // TAIL
    within = col % TAIL
    source = jnp.zeros_like(slot)
    for i, off in enumerate(OFFSETS):
        source = jnp.where(slot // cores == i, lax.rem(x + xs - off, xs), source)
    kpos = z * per_z + (source * cores + slot % cores) * rows + within
    real = (within < rows) & (slot < len(shards))
    lane = lax.broadcasted_iota(jnp.int32, (zrows, width), 1)
    sub = lax.broadcasted_iota(jnp.int32, (zrows, width), 0)
    tail_row = lax.broadcasted_iota(jnp.int32, (TAIL, width), 0)
    new_frame = (cache_frames + z * per_z // FRAME).astype(jnp.float32)
    filler = jnp.zeros((width - len(shards) * TAIL, width), jnp.float32)

    def tails(side, h):
        parts = [ref[a, side, h, keys:, :].astype(jnp.float32) for ref, a in shards]
        return parts, jnp.concatenate(parts + [filler], axis=0).astype(jnp.bfloat16)

    for b in range(zs // zb):
        qpos = (b * zb + row // zrows) * per_z + (x * cores + c) * rows + (row // group) % rows
        visible = real & (kpos <= qpos)
        qframe = float(cache_frames + b)
        lse_rows = jnp.zeros((zb, width), jnp.float32)
        q_all = q_ref[b * zb : (b + 1) * zb].astype(jnp.float32).reshape(zb * rows, heads, width)
        for h in range(groups):
            slope = slope_ref[h]
            q = q_all[:, h * group : (h + 1) * group, :].reshape(block, width).astype(jnp.bfloat16)
            parts, k_new = tails(0, h)
            _, v_new = tails(1, h)
            scores = []
            for part, (ref, a) in zip(parts, shards):
                bias = slope * (qframe - part[rows : rows + 1, :]) * -LOG2E
                bias = jnp.concatenate([bias] * (keys // width), axis=1)
                s = lax.dot_general(q, ref[a, 0, h, :keys, :], (((1,), (1,)), ((), ())), preferred_element_type=jnp.float32)
                t = s.reshape(block // group, group, keys) * scale + bias[None]
                scores.append(t.reshape(block, keys))
            bias = slope * (qframe - new_frame) * -LOG2E
            s = lax.dot_general(q, k_new, (((1,), (1,)), ((), ())), preferred_element_type=jnp.float32)
            t = (s.reshape(block // group, group, width) * scale + bias[None]).reshape(block, width)
            t_new = jnp.where(visible, t, -1e30)
            top = functools.reduce(jnp.maximum, scores)
            top = functools.reduce(jnp.maximum, [top[:, i : i + width] for i in range(0, keys, width)])
            high = jnp.max(jnp.maximum(top, t_new), axis=1, keepdims=True)
            total = jnp.exp2(t_new - high)
            acc = jnp.dot(total.astype(jnp.bfloat16), v_new, preferred_element_type=jnp.float32)
            for t, (ref, a) in zip(scores, shards):
                p = jnp.exp2(t - high)
                for i in range(0, keys, width):
                    total = total + p[:, i : i + width]
                acc = acc + jnp.dot(p.astype(jnp.bfloat16), ref[a, 1, h, :keys, :], preferred_element_type=jnp.float32)
            total = jnp.sum(total, axis=1, keepdims=True)
            out = (acc / total).astype(jnp.bfloat16)
            out_ref[b * zb : (b + 1) * zb, h * zrows : (h + 1) * zrows, :] = out.reshape(zb, zrows, width)
            lse = jnp.broadcast_to(high + jnp.log2(total), (block, width)).reshape(zb, zrows, width)
            lse_rows = lse_rows + jnp.sum(jnp.where((sub + h * zrows == lane)[None], lse, 0.0), axis=1)
        first = lse_rows.astype(jnp.bfloat16).astype(jnp.float32)
        second = (lse_rows - first).astype(jnp.bfloat16).astype(jnp.float32)
        third = lse_rows - first - second
        for i in range(zb):
            tail = jnp.where(tail_row == 0, first[i : i + 1], 0.0)
            tail = jnp.where(tail_row == 1, second[i : i + 1], tail)
            tail = jnp.where(tail_row == 2, third[i : i + 1], tail)
            out_ref[b * zb + i, groups * zrows :, :] = tail.astype(jnp.bfloat16)


def merge(rows, groups, in_ref, out_ref, scratch):
    zs, _, width = in_ref.shape
    count = in_ref.shape[1] - TAIL
    group = count // (rows * groups)
    lse = []
    for s in range(zs):
        tail = in_ref[s, count:, :].astype(jnp.float32)
        lse.append(tail[0:1] + tail[1:2] + tail[2:3])
    lse = jnp.concatenate(lse, axis=0)
    weight = jnp.exp2(lse - jnp.max(lse, axis=0, keepdims=True))
    weight = weight / jnp.sum(weight, axis=0, keepdims=True)
    weight = jnp.concatenate([weight, jnp.zeros((width - zs, width), jnp.float32)], axis=0).T
    acc = jnp.zeros((count, width), jnp.float32)
    for s in range(zs):
        acc = acc + weight[:count, s : s + 1] * in_ref[s, :count, :].astype(jnp.float32)
    scratch[...] = acc.reshape(groups, rows, group, width)
    for h in range(groups):
        for g in range(group):
            at = (h * group + g) * width
            out_ref[:, at : at + width] = scratch[h, :, g, :].astype(jnp.bfloat16)


def on_device(queries, cache_keys, cache_values, new_keys, new_values, frame_of_slot, slopes):
    rows, heads, width = queries.shape
    _, groups, _ = cache_keys.shape
    group = heads // groups
    zs, xs, cs = (lax.axis_size(a) for a in ("z", "x", "c"))
    cache_frames = zs * xs * cs * frame_of_slot.shape[0]
    vmem = pl.BlockSpec(memory_space=pltpu.VMEM)

    frame = jnp.broadcast_to(frame_of_slot.astype(jnp.bfloat16)[0], (groups, TAIL - rows, width))

    def side(cached, new):
        return jnp.concatenate([cached.transpose(1, 0, 2), new.transpose(1, 0, 2), frame], axis=1)

    packed = jnp.stack([side(cache_keys, new_keys), side(cache_values, new_values)])
    landing = [packed]
    for off in OFFSETS[1:]:
        landing.append(shifted(packed, "x", off))
    q_all = spread(queries, "z")
    blocks = [lax.all_gather(value, "c") for value in landing]
    slope = jnp.broadcast_to(slopes.reshape(groups, group, 1), (groups, group, width))
    chunk = groups * group * rows + TAIL
    partial = pl.pallas_call(
        functools.partial(attend, cache_frames),
        out_shape=jax.ShapeDtypeStruct((zs, chunk, width), jnp.bfloat16),
        in_specs=[vmem] * 6,
        out_specs=vmem,
        compiler_params=pltpu.CompilerParams(vmem_limit_bytes=ATTEND_VMEM),
        name="attend",
    )(*blocks, q_all, slope)
    landed = lax.all_to_all(partial, "z", 0, 0)
    result = pl.pallas_call(
        functools.partial(merge, rows, groups),
        out_shape=jax.ShapeDtypeStruct((rows, heads * width), jnp.bfloat16),
        in_specs=[vmem],
        out_specs=vmem,
        scratch_shapes=[pltpu.VMEM((groups, rows, group, width), jnp.float32)],
        compiler_params=pltpu.CompilerParams(vmem_limit_bytes=MERGE_VMEM),
        name="merge",
    )(landed)
    return jnp.concatenate(list(spread(result, "head")), axis=1)


def solution(mesh):
    heads = mesh.devices.shape[1]
    fine = Mesh(mesh.devices.reshape(*GRID, heads), ("z", "x", "c", "head"))
    ctx = ("z", "x", "c")
    return jax.shard_map(
        on_device,
        mesh=fine,
        in_specs=(P(ctx, "head", None),) * 5 + (P(ctx), P("head")),
        out_specs=P(ctx, None),
        check_vma=False,
    )
```

```python
import functools
import math

import jax
import jax.numpy as jnp
from jax import lax
from jax.experimental import pallas as pl
from jax.experimental.pallas import tpu as pltpu
from jax.sharding import Mesh, PartitionSpec as P


FRAME = 256
TAIL = 8
OFFSETS = (0, 1, -1, 2)
LOG2E = math.log2(math.e)
GRID = (16, 4, 2)
Q_FIRST = 10
OUT_FIRST = 2
ATTEND_VMEM = 24 << 20
MERGE_VMEM = 4 << 20


def shifted(value, axis, steps):
    count = lax.axis_size(axis)
    pairs = [(source, (source + steps) % count) for source in range(count)]
    return lax.ppermute(value, axis, pairs)


def ring(axis, first):
    count = lax.axis_size(axis)
    return [(first + i) % count for i in range(count)]


def spread(value, axis, first=0):
    copies = jnp.broadcast_to(value, (lax.axis_size(axis), *value.shape))
    return lax.all_to_all(copies, axis, 0, 0, axis_index_groups=[ring(axis, first)])


def attend(cache_frames, kv0, kv1, kv2, kv3, q_ref, slope_ref, out_ref):
    kvs = (kv0, kv1, kv2, kv3)
    zs, rows, heads, width = q_ref.shape
    cores, _, groups, keys, _ = kv0.shape
    keys -= TAIL
    xs = len(kvs)
    group = heads // groups
    z, x, c = lax.axis_index("z"), lax.axis_index("x"), lax.axis_index("c")
    shards = [(ref, i) for ref in kvs for i in range(cores)]
    per_z = len(shards) * rows
    zb = FRAME // per_z
    zrows = rows * group
    block = zb * zrows
    scale = LOG2E / width**0.5

    row = lax.broadcasted_iota(jnp.int32, (block, width), 0)
    col = lax.broadcasted_iota(jnp.int32, (block, width), 1)
    slot = col // TAIL
    within = col % TAIL
    source = jnp.zeros_like(slot)
    for i, off in enumerate(OFFSETS):
        source = jnp.where(slot // cores == i, lax.rem(x + xs - off, xs), source)
    kpos = z * per_z + (source * cores + slot % cores) * rows + within
    real = (within < rows) & (slot < len(shards))
    lane = lax.broadcasted_iota(jnp.int32, (zrows, width), 1)
    sub = lax.broadcasted_iota(jnp.int32, (zrows, width), 0)
    tail_row = lax.broadcasted_iota(jnp.int32, (TAIL, width), 0)
    new_frame = (cache_frames + z * per_z // FRAME).astype(jnp.float32)
    filler = jnp.zeros((width - len(shards) * TAIL, width), jnp.float32)

    def tails(side, h):
        parts = [ref[a, side, h, keys:, :].astype(jnp.float32) for ref, a in shards]
        return parts, jnp.concatenate(parts + [filler], axis=0).astype(jnp.bfloat16)

    for b in range(zs // zb):
        qpos = (b * zb + row // zrows) * per_z + (x * cores + c) * rows + (row // group) % rows
        visible = real & (kpos <= qpos)
        qframe = float(cache_frames + b)
        lse_rows = jnp.zeros((zb, width), jnp.float32)
        q_at = [(b * zb + i - Q_FIRST) % zs for i in range(zb)]
        out_at = [(b * zb + i - OUT_FIRST) % zs for i in range(zb)]
        q_all = jnp.concatenate([q_ref[i].astype(jnp.float32) for i in q_at], axis=0)
        for h in range(groups):
            slope = slope_ref[h]
            q = q_all[:, h * group : (h + 1) * group, :].reshape(block, width).astype(jnp.bfloat16)
            parts, k_new = tails(0, h)
            _, v_new = tails(1, h)
            scores = []
            for part, (ref, a) in zip(parts, shards):
                bias = slope * (qframe - part[rows : rows + 1, :]) * -LOG2E
                bias = jnp.concatenate([bias] * (keys // width), axis=1)
                s = lax.dot_general(q, ref[a, 0, h, :keys, :], (((1,), (1,)), ((), ())), preferred_element_type=jnp.float32)
                t = s.reshape(block // group, group, keys) * scale + bias[None]
                scores.append(t.reshape(block, keys))
            bias = slope * (qframe - new_frame) * -LOG2E
            s = lax.dot_general(q, k_new, (((1,), (1,)), ((), ())), preferred_element_type=jnp.float32)
            t = (s.reshape(block // group, group, width) * scale + bias[None]).reshape(block, width)
            t_new = jnp.where(visible, t, -1e30)
            top = functools.reduce(jnp.maximum, scores)
            top = functools.reduce(jnp.maximum, [top[:, i : i + width] for i in range(0, keys, width)])
            high = jnp.max(jnp.maximum(top, t_new), axis=1, keepdims=True)
            total = jnp.exp2(t_new - high)
            acc = jnp.dot(total.astype(jnp.bfloat16), v_new, preferred_element_type=jnp.float32)
            for t, (ref, a) in zip(scores, shards):
                p = jnp.exp2(t - high)
                for i in range(0, keys, width):
                    total = total + p[:, i : i + width]
                acc = acc + jnp.dot(p.astype(jnp.bfloat16), ref[a, 1, h, :keys, :], preferred_element_type=jnp.float32)
            total = jnp.sum(total, axis=1, keepdims=True)
            out = (acc / total).astype(jnp.bfloat16)
            for i, at in enumerate(out_at):
                out_ref[at, h * zrows : (h + 1) * zrows, :] = out[i * zrows : (i + 1) * zrows, :]
            lse = jnp.broadcast_to(high + jnp.log2(total), (block, width)).reshape(zb, zrows, width)
            lse_rows = lse_rows + jnp.sum(jnp.where((sub + h * zrows == lane)[None], lse, 0.0), axis=1)
        first = lse_rows.astype(jnp.bfloat16).astype(jnp.float32)
        second = (lse_rows - first).astype(jnp.bfloat16).astype(jnp.float32)
        third = lse_rows - first - second
        for i, at in enumerate(out_at):
            tail = jnp.where(tail_row == 0, first[i : i + 1], 0.0)
            tail = jnp.where(tail_row == 1, second[i : i + 1], tail)
            tail = jnp.where(tail_row == 2, third[i : i + 1], tail)
            out_ref[at, groups * zrows :, :] = tail.astype(jnp.bfloat16)


def merge(rows, groups, in_ref, out_ref, scratch):
    zs, _, width = in_ref.shape
    count = in_ref.shape[1] - TAIL
    group = count // (rows * groups)
    lse = []
    for s in range(zs):
        tail = in_ref[s, count:, :].astype(jnp.float32)
        lse.append(tail[0:1] + tail[1:2] + tail[2:3])
    lse = jnp.concatenate(lse, axis=0)
    weight = jnp.exp2(lse - jnp.max(lse, axis=0, keepdims=True))
    weight = weight / jnp.sum(weight, axis=0, keepdims=True)
    weight = jnp.concatenate([weight, jnp.zeros((width - zs, width), jnp.float32)], axis=0).T
    acc = jnp.zeros((count, width), jnp.float32)
    for s in range(zs):
        acc = acc + weight[:count, s : s + 1] * in_ref[s, :count, :].astype(jnp.float32)
    scratch[...] = acc.reshape(groups, rows, group, width)
    for h in range(groups):
        for g in range(group):
            at = (h * group + g) * width
            out_ref[:, at : at + width] = scratch[h, :, g, :].astype(jnp.bfloat16)


def on_device(queries, cache_keys, cache_values, new_keys, new_values, frame_of_slot, slopes):
    rows, heads, width = queries.shape
    _, groups, _ = cache_keys.shape
    group = heads // groups
    zs, xs, cs = (lax.axis_size(a) for a in ("z", "x", "c"))
    cache_frames = zs * xs * cs * frame_of_slot.shape[0]
    vmem = pl.BlockSpec(memory_space=pltpu.VMEM)

    frame = jnp.broadcast_to(frame_of_slot.astype(jnp.bfloat16)[0], (groups, TAIL - rows, width))

    def side(cached, new):
        return jnp.concatenate([cached.transpose(1, 0, 2), new.transpose(1, 0, 2), frame], axis=1)

    packed = jnp.stack([side(cache_keys, new_keys), side(cache_values, new_values)])
    landing = [packed]
    for off in OFFSETS[1:]:
        landing.append(shifted(packed, "x", off))
    q_all = spread(queries, "z", Q_FIRST)
    blocks = [lax.all_gather(value, "c") for value in landing]
    slope = jnp.broadcast_to(slopes.reshape(groups, group, 1), (groups, group, width))
    chunk = groups * group * rows + TAIL
    partial = pl.pallas_call(
        functools.partial(attend, cache_frames),
        out_shape=jax.ShapeDtypeStruct((zs, chunk, width), jnp.bfloat16),
        in_specs=[vmem] * 6,
        out_specs=vmem,
        compiler_params=pltpu.CompilerParams(vmem_limit_bytes=ATTEND_VMEM),
        name="attend",
    )(*blocks, q_all, slope)
    landed = lax.all_to_all(partial, "z", 0, 0, axis_index_groups=[ring("z", OUT_FIRST)])
    result = pl.pallas_call(
        functools.partial(merge, rows, groups),
        out_shape=jax.ShapeDtypeStruct((rows, heads * width), jnp.bfloat16),
        in_specs=[vmem],
        out_specs=vmem,
        scratch_shapes=[pltpu.VMEM((groups, rows, group, width), jnp.float32)],
        compiler_params=pltpu.CompilerParams(vmem_limit_bytes=MERGE_VMEM),
        name="merge",
    )(landed)
    return jnp.concatenate(list(spread(result, "head")), axis=1)


def solution(mesh):
    heads = mesh.devices.shape[1]
    fine = Mesh(mesh.devices.reshape(*GRID, heads), ("z", "x", "c", "head"))
    ctx = ("z", "x", "c")
    return jax.shard_map(
        on_device,
        mesh=fine,
        in_specs=(P(ctx, "head", None),) * 5 + (P(ctx), P("head")),
        out_specs=P(ctx, None),
        check_vma=False,
    )
```

```python
import functools
import math

import jax
import jax.numpy as jnp
from jax import lax
from jax.experimental import pallas as pl
from jax.experimental.pallas import tpu as pltpu
from jax.sharding import Mesh, PartitionSpec as P


FRAME = 256
TAIL = 8
OFFSETS = (0, -1, 1, 2)
LOG2E = math.log2(math.e)
GRID = (16, 4, 2)
Q_FIRST = 8
OUT_FIRST = 0
HEAD_FIRST = 3
ATTEND_VMEM = 24 << 20
MERGE_VMEM = 4 << 20


def shifted(value, axis, steps):
    count = lax.axis_size(axis)
    pairs = [(source, (source + steps) % count) for source in range(count)]
    return lax.ppermute(value, axis, pairs)


def ring(axis, first):
    count = lax.axis_size(axis)
    return [(first + i) % count for i in range(count)]


def spread(value, axis, first=0):
    copies = jnp.broadcast_to(value, (lax.axis_size(axis), *value.shape))
    return lax.all_to_all(copies, axis, 0, 0, axis_index_groups=[ring(axis, first)])


def attend(cache_frames, kv0, kv1, kv2, kv3, q_ref, slope_ref, out_ref):
    kvs = (kv0, kv1, kv2, kv3)
    zs, rows, heads, width = q_ref.shape
    cores, _, groups, keys, _ = kv0.shape
    keys -= TAIL
    xs = len(kvs)
    group = heads // groups
    z, x, c = lax.axis_index("z"), lax.axis_index("x"), lax.axis_index("c")
    shards = [(ref, i) for ref in kvs for i in range(cores)]
    per_z = len(shards) * rows
    zb = FRAME // per_z
    zrows = rows * group
    block = zb * zrows
    scale = LOG2E / width**0.5

    row = lax.broadcasted_iota(jnp.int32, (block, width), 0)
    col = lax.broadcasted_iota(jnp.int32, (block, width), 1)
    slot = col // TAIL
    within = col % TAIL
    source = jnp.zeros_like(slot)
    for i, off in enumerate(OFFSETS):
        source = jnp.where(slot // cores == i, lax.rem(x + xs - off, xs), source)
    kpos = z * per_z + (source * cores + slot % cores) * rows + within
    real = (within < rows) & (slot < len(shards))
    lane = lax.broadcasted_iota(jnp.int32, (zrows, width), 1)
    sub = lax.broadcasted_iota(jnp.int32, (zrows, width), 0)
    tail_row = lax.broadcasted_iota(jnp.int32, (TAIL, width), 0)
    new_frame = (cache_frames + z * per_z // FRAME).astype(jnp.float32)
    filler = jnp.zeros((width - len(shards) * TAIL, width), jnp.float32)

    def tails(side, h):
        parts = [ref[a, side, h, keys:, :].astype(jnp.float32) for ref, a in shards]
        return parts, jnp.concatenate(parts + [filler], axis=0).astype(jnp.bfloat16)

    for b in range(zs // zb):
        qpos = (b * zb + row // zrows) * per_z + (x * cores + c) * rows + (row // group) % rows
        visible = real & (kpos <= qpos)
        qframe = float(cache_frames + b)
        lse_rows = jnp.zeros((zb, width), jnp.float32)
        q_at = [(b * zb + i - Q_FIRST) % zs for i in range(zb)]
        out_at = [(b * zb + i - OUT_FIRST) % zs for i in range(zb)]
        q_all = jnp.concatenate([q_ref[i].astype(jnp.float32) for i in q_at], axis=0)
        for h in range(groups):
            slope = slope_ref[h]
            q = q_all[:, h * group : (h + 1) * group, :].reshape(block, width).astype(jnp.bfloat16)
            parts, k_new = tails(0, h)
            _, v_new = tails(1, h)
            scores = []
            for part, (ref, a) in zip(parts, shards):
                bias = slope * (qframe - part[rows : rows + 1, :]) * -LOG2E
                bias = jnp.concatenate([bias] * (keys // width), axis=1)
                s = lax.dot_general(q, ref[a, 0, h, :keys, :], (((1,), (1,)), ((), ())), preferred_element_type=jnp.float32)
                t = s.reshape(block // group, group, keys) * scale + bias[None]
                scores.append(t.reshape(block, keys))
            bias = slope * (qframe - new_frame) * -LOG2E
            s = lax.dot_general(q, k_new, (((1,), (1,)), ((), ())), preferred_element_type=jnp.float32)
            t = (s.reshape(block // group, group, width) * scale + bias[None]).reshape(block, width)
            t_new = jnp.where(visible, t, -1e30)
            top = functools.reduce(jnp.maximum, scores)
            top = functools.reduce(jnp.maximum, [top[:, i : i + width] for i in range(0, keys, width)])
            high = jnp.max(jnp.maximum(top, t_new), axis=1, keepdims=True)
            total = jnp.exp2(t_new - high)
            acc = jnp.dot(total.astype(jnp.bfloat16), v_new, preferred_element_type=jnp.float32)
            for t, (ref, a) in zip(scores, shards):
                p = jnp.exp2(t - high)
                for i in range(0, keys, width):
                    total = total + p[:, i : i + width]
                acc = acc + jnp.dot(p.astype(jnp.bfloat16), ref[a, 1, h, :keys, :], preferred_element_type=jnp.float32)
            total = jnp.sum(total, axis=1, keepdims=True)
            out = (acc / total).astype(jnp.bfloat16)
            for i, at in enumerate(out_at):
                out_ref[at, h * zrows : (h + 1) * zrows, :] = out[i * zrows : (i + 1) * zrows, :]
            lse = jnp.broadcast_to(high + jnp.log2(total), (block, width)).reshape(zb, zrows, width)
            lse_rows = lse_rows + jnp.sum(jnp.where((sub + h * zrows == lane)[None], lse, 0.0), axis=1)
        first = lse_rows.astype(jnp.bfloat16).astype(jnp.float32)
        second = (lse_rows - first).astype(jnp.bfloat16).astype(jnp.float32)
        third = lse_rows - first - second
        for i, at in enumerate(out_at):
            tail = jnp.where(tail_row == 0, first[i : i + 1], 0.0)
            tail = jnp.where(tail_row == 1, second[i : i + 1], tail)
            tail = jnp.where(tail_row == 2, third[i : i + 1], tail)
            out_ref[at, groups * zrows :, :] = tail.astype(jnp.bfloat16)


def merge(rows, groups, in_ref, out_ref, scratch):
    zs, _, width = in_ref.shape
    count = in_ref.shape[1] - TAIL
    group = count // (rows * groups)
    lse = []
    for s in range(zs):
        tail = in_ref[s, count:, :].astype(jnp.float32)
        lse.append(tail[0:1] + tail[1:2] + tail[2:3])
    lse = jnp.concatenate(lse, axis=0)
    weight = jnp.exp2(lse - jnp.max(lse, axis=0, keepdims=True))
    weight = weight / jnp.sum(weight, axis=0, keepdims=True)
    weight = jnp.concatenate([weight, jnp.zeros((width - zs, width), jnp.float32)], axis=0).T
    acc = jnp.zeros((count, width), jnp.float32)
    for s in range(zs):
        acc = acc + weight[:count, s : s + 1] * in_ref[s, :count, :].astype(jnp.float32)
    scratch[...] = acc.reshape(groups, rows, group, width)
    for h in range(groups):
        for g in range(group):
            at = (h * group + g) * width
            out_ref[:, at : at + width] = scratch[h, :, g, :].astype(jnp.bfloat16)


def on_device(queries, cache_keys, cache_values, new_keys, new_values, frame_of_slot, slopes):
    rows, heads, width = queries.shape
    _, groups, _ = cache_keys.shape
    group = heads // groups
    zs, xs, cs = (lax.axis_size(a) for a in ("z", "x", "c"))
    cache_frames = zs * xs * cs * frame_of_slot.shape[0]
    vmem = pl.BlockSpec(memory_space=pltpu.VMEM)

    frame = jnp.broadcast_to(frame_of_slot.astype(jnp.bfloat16)[0], (groups, TAIL - rows, width))

    def side(cached, new):
        return jnp.concatenate([cached.transpose(1, 0, 2), new.transpose(1, 0, 2), frame], axis=1)

    packed = jnp.stack([side(cache_keys, new_keys), side(cache_values, new_values)])
    landing = [packed]
    for off in OFFSETS[1:]:
        landing.append(shifted(packed, "x", off))
    q_all = spread(queries, "z", Q_FIRST)
    blocks = [lax.all_gather(value, "c") for value in landing]
    slope = jnp.broadcast_to(slopes.reshape(groups, group, 1), (groups, group, width))
    chunk = groups * group * rows + TAIL
    partial = pl.pallas_call(
        functools.partial(attend, cache_frames),
        out_shape=jax.ShapeDtypeStruct((zs, chunk, width), jnp.bfloat16),
        in_specs=[vmem] * 6,
        out_specs=vmem,
        compiler_params=pltpu.CompilerParams(vmem_limit_bytes=ATTEND_VMEM),
        name="attend",
    )(*blocks, q_all, slope)
    landed = lax.all_to_all(partial, "z", 0, 0, axis_index_groups=[ring("z", OUT_FIRST)])
    result = pl.pallas_call(
        functools.partial(merge, rows, groups),
        out_shape=jax.ShapeDtypeStruct((rows, heads * width), jnp.bfloat16),
        in_specs=[vmem],
        out_specs=vmem,
        scratch_shapes=[pltpu.VMEM((groups, rows, group, width), jnp.float32)],
        compiler_params=pltpu.CompilerParams(vmem_limit_bytes=MERGE_VMEM),
        name="merge",
    )(landed)
    parts = spread(result, "head", HEAD_FIRST)
    return jnp.concatenate([parts[ring("head", HEAD_FIRST).index(i)] for i in range(len(parts))], axis=1)


def solution(mesh):
    heads = mesh.devices.shape[1]
    fine = Mesh(mesh.devices.reshape(*GRID, heads), ("z", "x", "c", "head"))
    ctx = ("z", "x", "c")
    return jax.shard_map(
        on_device,
        mesh=fine,
        in_specs=(P(ctx, "head", None),) * 5 + (P(ctx), P("head")),
        out_specs=P(ctx, None),
        check_vma=False,
    )
```

```python
import functools
import math

import jax
import jax.numpy as jnp
from jax import lax
from jax.experimental import pallas as pl
from jax.experimental.pallas import tpu as pltpu
from jax.sharding import Mesh, PartitionSpec as P


FRAME = 256
TAIL = 8
OFFSETS = (0, -1, 1, 2)
LOG2E = math.log2(math.e)
GRID = (16, 4, 2)
Q_FIRST = 9
OUT_FIRST = 15
HEAD_FIRST = 1
ATTEND_VMEM = 24 << 20
MERGE_VMEM = 4 << 20


def shifted(value, axis, steps):
    count = lax.axis_size(axis)
    pairs = [(source, (source + steps) % count) for source in range(count)]
    return lax.ppermute(value, axis, pairs)


def ring(axis, first):
    count = lax.axis_size(axis)
    return [(first + i) % count for i in range(count)]


def spread(value, axis, first=0):
    copies = jnp.broadcast_to(value, (lax.axis_size(axis), *value.shape))
    return lax.all_to_all(copies, axis, 0, 0, axis_index_groups=[ring(axis, first)])


def attend(cache_frames, kv0, kv1, kv2, kv3, q_ref, slope_ref, out_ref):
    kvs = (kv0, kv1, kv2, kv3)
    zs, rows, heads, width = q_ref.shape
    cores, _, groups, keys, _ = kv0.shape
    keys -= TAIL
    xs = len(kvs)
    group = heads // groups
    z, x, c = lax.axis_index("z"), lax.axis_index("x"), lax.axis_index("c")
    shards = [(ref, i) for ref in kvs for i in range(cores)]
    per_z = len(shards) * rows
    zb = FRAME // per_z
    zrows = rows * group
    block = zb * zrows
    scale = LOG2E / width**0.5

    row = lax.broadcasted_iota(jnp.int32, (block, width), 0)
    col = lax.broadcasted_iota(jnp.int32, (block, width), 1)
    slot = col // TAIL
    within = col % TAIL
    source = jnp.zeros_like(slot)
    for i, off in enumerate(OFFSETS):
        source = jnp.where(slot // cores == i, lax.rem(x + xs - off, xs), source)
    kpos = z * per_z + (source * cores + slot % cores) * rows + within
    real = (within < rows) & (slot < len(shards))
    lane = lax.broadcasted_iota(jnp.int32, (zrows, width), 1)
    sub = lax.broadcasted_iota(jnp.int32, (zrows, width), 0)
    tail_row = lax.broadcasted_iota(jnp.int32, (TAIL, width), 0)
    new_frame = (cache_frames + z * per_z // FRAME).astype(jnp.float32)
    filler = jnp.zeros((width - len(shards) * TAIL, width), jnp.float32)

    def tails(side, h):
        parts = [ref[a, side, h, keys:, :].astype(jnp.float32) for ref, a in shards]
        return parts, jnp.concatenate(parts + [filler], axis=0).astype(jnp.bfloat16)

    for b in range(zs // zb):
        qpos = (b * zb + row // zrows) * per_z + (x * cores + c) * rows + (row // group) % rows
        visible = real & (kpos <= qpos)
        qframe = float(cache_frames + b)
        lse_rows = jnp.zeros((zb, width), jnp.float32)
        q_at = [(b * zb + i - Q_FIRST) % zs for i in range(zb)]
        out_at = [(b * zb + i - OUT_FIRST) % zs for i in range(zb)]
        q_all = jnp.concatenate([q_ref[i].astype(jnp.float32) for i in q_at], axis=0)
        for h in range(groups):
            slope = slope_ref[h]
            q = q_all[:, h * group : (h + 1) * group, :].reshape(block, width).astype(jnp.bfloat16)
            parts, k_new = tails(0, h)
            _, v_new = tails(1, h)
            scores = []
            for part, (ref, a) in zip(parts, shards):
                bias = slope * (qframe - part[rows : rows + 1, :]) * -LOG2E
                bias = jnp.concatenate([bias] * (keys // width), axis=1)
                s = lax.dot_general(q, ref[a, 0, h, :keys, :], (((1,), (1,)), ((), ())), preferred_element_type=jnp.float32)
                t = s.reshape(block // group, group, keys) * scale + bias[None]
                scores.append(t.reshape(block, keys))
            bias = slope * (qframe - new_frame) * -LOG2E
            s = lax.dot_general(q, k_new, (((1,), (1,)), ((), ())), preferred_element_type=jnp.float32)
            t = (s.reshape(block // group, group, width) * scale + bias[None]).reshape(block, width)
            t_new = jnp.where(visible, t, -1e30)
            top = functools.reduce(jnp.maximum, scores)
            top = functools.reduce(jnp.maximum, [top[:, i : i + width] for i in range(0, keys, width)])
            high = jnp.max(jnp.maximum(top, t_new), axis=1, keepdims=True)
            total = jnp.exp2(t_new - high)
            acc = jnp.dot(total.astype(jnp.bfloat16), v_new, preferred_element_type=jnp.float32)
            for t, (ref, a) in zip(scores, shards):
                p = jnp.exp2(t - high)
                for i in range(0, keys, width):
                    total = total + p[:, i : i + width]
                acc = acc + jnp.dot(p.astype(jnp.bfloat16), ref[a, 1, h, :keys, :], preferred_element_type=jnp.float32)
            total = jnp.sum(total, axis=1, keepdims=True)
            out = (acc / total).astype(jnp.bfloat16)
            for i, at in enumerate(out_at):
                out_ref[at, h * zrows : (h + 1) * zrows, :] = out[i * zrows : (i + 1) * zrows, :]
            lse = jnp.broadcast_to(high + jnp.log2(total), (block, width)).reshape(zb, zrows, width)
            lse_rows = lse_rows + jnp.sum(jnp.where((sub + h * zrows == lane)[None], lse, 0.0), axis=1)
        first = lse_rows.astype(jnp.bfloat16).astype(jnp.float32)
        second = (lse_rows - first).astype(jnp.bfloat16).astype(jnp.float32)
        third = lse_rows - first - second
        for i, at in enumerate(out_at):
            tail = jnp.where(tail_row == 0, first[i : i + 1], 0.0)
            tail = jnp.where(tail_row == 1, second[i : i + 1], tail)
            tail = jnp.where(tail_row == 2, third[i : i + 1], tail)
            out_ref[at, groups * zrows :, :] = tail.astype(jnp.bfloat16)


def merge(rows, groups, in_ref, out_ref, scratch):
    zs, _, width = in_ref.shape
    count = in_ref.shape[1] - TAIL
    group = count // (rows * groups)
    lse = []
    for s in range(zs):
        tail = in_ref[s, count:, :].astype(jnp.float32)
        lse.append(tail[0:1] + tail[1:2] + tail[2:3])
    lse = jnp.concatenate(lse, axis=0)
    weight = jnp.exp2(lse - jnp.max(lse, axis=0, keepdims=True))
    weight = weight / jnp.sum(weight, axis=0, keepdims=True)
    weight = jnp.concatenate([weight, jnp.zeros((width - zs, width), jnp.float32)], axis=0).T
    acc = jnp.zeros((count, width), jnp.float32)
    for s in range(zs):
        acc = acc + weight[:count, s : s + 1] * in_ref[s, :count, :].astype(jnp.float32)
    scratch[...] = acc.reshape(groups, rows, group, width)
    for h in range(groups):
        for g in range(group):
            at = (h * group + g) * width
            out_ref[:, at : at + width] = scratch[h, :, g, :].astype(jnp.bfloat16)


def on_device(queries, cache_keys, cache_values, new_keys, new_values, frame_of_slot, slopes):
    rows, heads, width = queries.shape
    _, groups, _ = cache_keys.shape
    group = heads // groups
    zs, xs, cs = (lax.axis_size(a) for a in ("z", "x", "c"))
    cache_frames = zs * xs * cs * frame_of_slot.shape[0]
    vmem = pl.BlockSpec(memory_space=pltpu.VMEM)

    frame = jnp.broadcast_to(frame_of_slot.astype(jnp.bfloat16)[0], (groups, TAIL - rows, width))

    def side(cached, new):
        return jnp.concatenate([cached.transpose(1, 0, 2), new.transpose(1, 0, 2), frame], axis=1)

    packed = jnp.stack([side(cache_keys, new_keys), side(cache_values, new_values)])
    landing = [packed]
    for off in OFFSETS[1:]:
        landing.append(shifted(packed, "x", off))
    q_all = spread(queries, "z", Q_FIRST)
    blocks = [lax.all_gather(value, "c") for value in landing]
    slope = jnp.broadcast_to(slopes.reshape(groups, group, 1), (groups, group, width))
    chunk = groups * group * rows + TAIL
    partial = pl.pallas_call(
        functools.partial(attend, cache_frames),
        out_shape=jax.ShapeDtypeStruct((zs, chunk, width), jnp.bfloat16),
        in_specs=[vmem] * 6,
        out_specs=vmem,
        compiler_params=pltpu.CompilerParams(vmem_limit_bytes=ATTEND_VMEM),
        name="attend",
    )(*blocks, q_all, slope)
    landed = lax.all_to_all(partial, "z", 0, 0, axis_index_groups=[ring("z", OUT_FIRST)])
    result = pl.pallas_call(
        functools.partial(merge, rows, groups),
        out_shape=jax.ShapeDtypeStruct((rows, heads * width), jnp.bfloat16),
        in_specs=[vmem],
        out_specs=vmem,
        scratch_shapes=[pltpu.VMEM((groups, rows, group, width), jnp.float32)],
        compiler_params=pltpu.CompilerParams(vmem_limit_bytes=MERGE_VMEM),
        name="merge",
    )(landed)
    parts = spread(result, "head", HEAD_FIRST)
    return jnp.concatenate([parts[ring("head", HEAD_FIRST).index(i)] for i in range(len(parts))], axis=1)


def solution(mesh):
    heads = mesh.devices.shape[1]
    fine = Mesh(mesh.devices.reshape(*GRID, heads), ("z", "x", "c", "head"))
    ctx = ("z", "x", "c")
    return jax.shard_map(
        on_device,
        mesh=fine,
        in_specs=(P(ctx, "head", None),) * 5 + (P(ctx), P("head")),
        out_specs=P(ctx, None),
        check_vma=False,
    )
```
